32 devices in a mesh: view: 4 (over z), patch: 8 (over y, x, core).
Axes of the slice: x: 2, y: 2, z: 4, core: 2. Of those that a mesh axis runs over, the one named last changes fastest.
Arguments:
- coefficients: bfloat16 [8, 2304, 32, 512], P('view', 'patch'), may hold values from -0.1875 to 0.1875
- sky_year: bfloat16 [2304, 8760], P('patch'), may hold values from 0.19921875 to 5
- hour_list: int32 [96], replicated, may hold values from 0 to 8759
- retention: float32 [32, 512], P('patch'), may hold values from 0 to 1
Outputs:
- acuity: float32 [32, 8, 96, 512], P('patch', 'view')
- veil: float32 [32, 8, 96, 512], P('patch', 'view')
The draws below stay inside these ranges and needn't reach their ends.
All inputs are finite; a program needn't handle non-finite values.
Results may differ from the reference program's by a relative error of at most 0.0003.
Values may be sent and summed in bfloat16 or wider, within the bound.
A program may use at most 128 MiB of HBM per device.

```python
import math
import jax
import jax.numpy as jnp
from jax import lax

VIEWS = 8
PATCHES = 2304
COLS = 512
HOURS = 96
YEAR = 8760
STRIP_LINE_COUNT = 32


def draw_retention(key, part):
    key_rate, key_rough, marker_image_lines, key_depth = jax.random.split(key, 4)
    spread = jax.random.uniform(key_rate, (COLS,), jnp.float32, math.log(0.3), math.log(40.0))
    strength = jnp.exp(spread)
    roughness = jax.random.uniform(key_rough, (STRIP_LINE_COUNT, COLS), jnp.float32, 0.5, 1.5)
    dazzle_spike_lines = jax.random.randint(marker_image_lines, (3,), 0, STRIP_LINE_COUNT)
    sample_locations = jnp.arange(STRIP_LINE_COUNT, dtype=jnp.int32)
    lit_sample_spots = jnp.any(sample_locations[:, None] == dazzle_spike_lines[None, :], axis=1)
    depths = jax.random.uniform(key_depth, (STRIP_LINE_COUNT, COLS), jnp.float32, 0.5, 0.8)
    factor = jnp.where(lit_sample_spots[:, None], depths, jnp.float32(1.0))
    return jnp.exp(-strength[None, :] * roughness / STRIP_LINE_COUNT) * factor


def place_ends(array, stream_key, low, top_value):
    shape = array.shape
    index_at = [jax.random.randint(jax.random.fold_in(stream_key, axis), (), 0, shape[axis]) for axis in range(len(shape))]
    array = array.at[tuple(index_at)].set(low)
    longest = shape.index(max(shape))
    index_at[longest] = (index_at[longest] + 1) % shape[longest]
    return array.at[tuple(index_at)].set(top_value)


def with_spikes(drawn, own_key, source, target, shards_of, factor):
    owner, partner = [(jnp.arange(drawn.shape[axis_at]) // (drawn.shape[axis_at] // shards_of)).reshape([-1 if axis == axis_at else 1 for axis in range(drawn.ndim)]) for axis_at in (source, target)]
    chosen = jax.random.permutation(own_key, shards_of)[partner]
    strong = (owner == chosen) | (owner == (partner + shards_of // 2) % shards_of)
    return jnp.where(strong, factor * drawn, drawn)


def levels(own_key, shape, cuts, smallest, high):
    level, own = 1.0, jax.random.fold_in(own_key, 6)
    for dim, parts in cuts:
        draws = jnp.exp(jax.random.uniform(jax.random.fold_in(own, dim), (parts,), jnp.float32, smallest / len(cuts), high / len(cuts)))
        level = level * jnp.repeat(draws, shape[dim] // parts).reshape([-1 if axis == dim else 1 for axis in range(len(shape))])
    return level


def heavy_noise(key, extent, scale, limit, cuts, heavy, held_as=jnp.bfloat16):
    values = scale * jax.random.normal(key, extent, jnp.float32)
    if cuts:
        values = values * levels(key, extent, cuts, -0.22, 0.18)
    return jnp.clip(with_spikes(values, jax.random.fold_in(key, 3), *heavy), -limit, limit).astype(held_as)


def setup_inputs(seed: int = 0) -> dict:
    arg_keys = jax.random.split(jax.random.key(seed), 5)
    coefficients = heavy_noise(arg_keys[0], (VIEWS, PATCHES, STRIP_LINE_COUNT, COLS), PATCHES ** -0.5, 0.1875, ((0, 4), (1, 8)), (1, 2, 8, 2.0))
    sky_year = jnp.clip(jnp.exp(math.log(5.0) - 3.2227897 * jax.random.uniform(arg_keys[1], (PATCHES, YEAR), jnp.float32) ** levels(arg_keys[1], (PATCHES, YEAR), ((0, 8),), -0.2, 0.2)), 0.19921875, 5.0).astype(jnp.bfloat16)
    hour_list = place_ends(jax.random.randint(arg_keys[2], (HOURS,), 0, YEAR), jax.random.fold_in(arg_keys[2], 1), 0, YEAR - 1).astype(jnp.int32)
    retention = draw_retention(jax.random.fold_in(arg_keys[4], 71), 0)
    return {"coefficients": coefficients, "sky_year": sky_year, "hour_list": hour_list, "retention": retention}


binomial_taps = (0.0625, 0.25, 0.375, 0.25, 0.0625)


def pascal_kernel(field, device_axis_name):
    size = field.shape[device_axis_name]
    widths = [(0, 0)] * field.ndim
    widths[device_axis_name] = (2, 2)
    padded = jnp.pad(field, widths)
    total = jnp.zeros_like(field)
    for offset in range(5):
        total = total + binomial_taps[offset] * lax.slice_in_dim(padded, offset, offset + size, axis=device_axis_name)
    return total


def reference(coefficients, sky_year, hour_list, retention):
    sky = jnp.take(sky_year, hour_list, axis=1)
    sky_rows = sky.T

    def render(single_view):
        flat = single_view.reshape(single_view.shape[0], -1)
        return jnp.dot(sky_rows, flat, preferred_element_type=jnp.float32).reshape(sky_rows.shape[0], single_view.shape[1], single_view.shape[2])

    images = lax.map(render, coefficients)
    luminance = jnp.transpose(images, (2, 0, 1, 3))
    across = pascal_kernel(luminance, 3)
    acuity = pascal_kernel(across, 0)

    def advance(state, inputs):
        carried = inputs[0][None, None, :] * state + inputs[1]
        return carried, carried

    initial_state = jnp.zeros(luminance.shape[1:], jnp.float32)
    _, forward = lax.scan(advance, initial_state, (retention, luminance))
    _, reverse_pass = lax.scan(advance, initial_state, (retention, luminance), reverse=True)
    veil = 0.125 * (forward + reverse_pass)
    return acuity, veil
```

```python
import jax
import jax.numpy as jnp
from jax import lax
from jax.experimental import pallas as pl
from jax.experimental.pallas import tpu as pltpu
from jax.sharding import PartitionSpec as P

binomial_taps = (0.0625, 0.25, 0.375, 0.25, 0.0625)
MESH = pl.DeviceIdType.MESH
SPAN = 83.0


def padded_2(block, sides, width):
    for axis, dim in sides:
        count = lax.axis_size(axis)
        forward = [(i, i + 1) for i in range(count - 1)]
        backward = [(target, source) for source, target in forward]
        low = lax.ppermute(
            lax.slice_in_dim(block, block.shape[dim] - width, None, axis=dim), axis, forward
        )
        high = lax.ppermute(lax.slice_in_dim(block, 0, width, axis=dim), axis, backward)
        block = jnp.concatenate([low, block, high], axis=dim)
    return block


def entering(value, axis, join, neutral, backward):
    count, mine = (lax.axis_size(axis), lax.axis_index(axis))
    pieces = jax.tree.map(lambda part: lax.all_gather(part, axis), value)
    if backward:
        pieces = jax.tree.map(lambda part: part[::-1], pieces)
        mine = count - 1 - mine
    running = jax.tree.map(
        lambda part, zero: jnp.full_like(part, 0) + jnp.asarray(zero, part.dtype), value, neutral
    )

    def hop(position, running):
        longer = join(running, jax.tree.map(lambda part: part[position], pieces))
        return jax.tree.map(lambda new, old: jnp.where(position < mine, new, old), longer, running)

    return lax.fori_loop(0, count - 1, hop, running)


def combine(earlier, later):
    return (earlier[0] * later[0], later[0] * earlier[1] + later[1])


def taps_sum(padded, axis, length):
    total = jnp.zeros(
        padded.shape[:axis] + (length,) + padded.shape[axis + 1 :],
        jnp.float32,
    )
    for offset in range(5):
        total = total + binomial_taps[offset] * lax.slice_in_dim(
            padded, offset, offset + length, axis=axis
        )
    return total


def general(coefficients, sky_year, hour_list, retention):
    sky_shard_values = jnp.take(sky_year, hour_list, axis=1)
    row_count = retention.shape[0]
    luminance = lax.psum_scatter(
        jnp.einsum(
            "ph,vprc->rvhc", sky_shard_values, coefficients, preferred_element_type=jnp.float32
        ),
        "patch",
        scatter_dimension=0,
        tiled=True,
    )
    padded = padded_2(luminance, (("patch", 0),), 2)
    image_width = padded.shape[3]
    wide_pad = jnp.pad(padded, ((0, 0), (0, 0), (0, 0), (2, 2)))
    across = taps_sum(wide_pad, 3, image_width)
    acuity = taps_sum(across, 0, row_count)
    retain_rates = retention[:, None, None, :]
    front_gain, front_sum = lax.associative_scan(combine, (retain_rates, luminance), axis=0)
    unity = (jnp.ones_like(front_gain[-1]), jnp.zeros_like(front_sum[-1]))
    _, incoming_down = entering((front_gain[-1], front_sum[-1]), "patch", combine, unity, False)
    forward = front_gain * incoming_down[None] + front_sum
    back_gain, back_sum = lax.associative_scan(
        combine, (retain_rates, luminance), reverse=True, axis=0
    )
    _, incoming_up = entering((back_gain[0], back_sum[0]), "patch", combine, unity, True)
    reverse_pass = back_gain * incoming_up[None] + back_sum
    veil = 0.125 * (forward + reverse_pass)
    return (acuity, veil)


def encode(x):
    top = jnp.maximum(jnp.max(jnp.abs(x), axis=0, keepdims=True), 1e-30)
    size = jnp.exp(jnp.abs(x) * (2.0 * SPAN / top) - SPAN)
    return jnp.where(x < 0, -size, size).astype(jnp.bfloat16), top


def decode(code, top):
    y = code.astype(jnp.float32)
    size = (jnp.log(jnp.abs(y)) + SPAN) * (top * (0.5 / SPAN))
    return jnp.where(y < 0, -size, size)


def kernel(
    sky_ref, coef_ref, ret_ref, acu_out, veil_out,
    lhs, held, mine, given, taken,
    code_out, top_out, code_in, top_in, lum,
    halo_out, halo_top_out, halo_in, halo_top_in,
    carry_out, carry_top_out, carry_in, carry_top_in,
    rets, down, acuity, veil,
    load_sem, ret_sem, pair_sem, hop_sem, halo_sem, carry_sem, out_sem, local_sem,
):
    view = lax.axis_index("view")
    me = lax.axis_index("patch")
    devices = 8
    chips = 4
    core = me % 2
    chip = me // 2
    cx = chip % 2
    cy = chip // 2
    other = 1 - core
    depth, rows, columns = held.shape[1:]
    hours = sky_ref.shape[0]

    def at(target):
        return (view, target)

    def chip_of(k, owner):
        fx = (1 - owner) * (1 - k // 2) + owner * (1 - k % 2)
        fy = owner * (1 - k // 2) + (1 - owner) * (1 - k % 2)
        return 2 * (cy + fy * (1 - 2 * cy)) + cx + fx * (1 - 2 * cx)

    def load(v, d, slot):
        return pltpu.make_async_copy(
            coef_ref.at[v, :, pl.ds(pl.multiple_of(d * rows, rows), rows), :],
            held.at[slot],
            load_sem.at[slot],
        )

    load(other, chip_of(0, other), 0).start()
    load(core, chip_of(0, core), 1).start()

    barrier = pltpu.get_barrier_semaphore()
    for step in range(1, devices):
        pl.semaphore_signal(
            barrier, inc=1, device_id=at((me + step) % devices), device_id_type=MESH
        )

    spread = (
        lax.broadcasted_iota(jnp.int32, (depth, depth * rows), 1) // rows
        == lax.broadcasted_iota(jnp.int32, (depth, depth * rows), 0)
    )
    wide = jnp.dot(
        sky_ref[...],
        jnp.where(spread, 1.0, 0.0).astype(jnp.bfloat16),
        preferred_element_type=jnp.float32,
    )
    place = lax.broadcasted_iota(jnp.int32, (hours, depth * rows), 1) % rows
    for r in range(rows):
        lhs[r * hours : (r + 1) * hours, :] = jnp.where(place == r, wide, 0.0).astype(jnp.bfloat16)

    pl.semaphore_wait(barrier, devices - 1)

    rets[me] = ret_ref[...]
    ret_copies = []
    for step in range(1, devices):
        target = (me + step) % devices
        copy = pltpu.make_async_remote_copy(
            src_ref=ret_ref,
            dst_ref=rets.at[me],
            send_sem=ret_sem.at[0, step],
            recv_sem=ret_sem.at[1, step],
            device_id=at(target),
            device_id_type=MESH,
        )
        copy.start()
        ret_copies.append(copy)

    partner = chip * 2 + other
    tile = 256

    def product(slot, dst, k):
        @pl.loop(0, columns // tile)
        def _(t):
            cols = pl.ds(pl.multiple_of(t * tile, tile), tile)
            block = held[slot, :, :, cols].reshape(depth * rows, tile)
            dst[k, :, :, cols] = jnp.dot(
                lhs[...], block, preferred_element_type=jnp.float32
            ).reshape(rows, hours, tile)

    def pair(k):
        return pltpu.make_async_remote_copy(
            src_ref=given.at[k],
            dst_ref=taken.at[k],
            send_sem=pair_sem.at[0, k],
            recv_sem=pair_sem.at[1, k],
            device_id=at(partner),
            device_id_type=MESH,
        )

    def hop(k, n):
        target = chip_of(n, core) * 2 + core
        return [
            pltpu.make_async_remote_copy(
                src_ref=src.at[k],
                dst_ref=dst.at[k],
                send_sem=hop_sem.at[0, i, k],
                recv_sem=hop_sem.at[1, i, k],
                device_id=at(target),
                device_id_type=MESH,
            )
            for i, (src, dst) in enumerate(((code_out, code_in), (top_out, top_in)))
        ]

    @pl.loop(0, chips)
    def _(k):
        load(other, chip_of(k, other), 0).wait()
        product(0, given, k)
        pair(k).start()

        @pl.when(k < chips - 1)
        def _():
            load(other, chip_of(k + 1, other), 0).start()

        load(core, chip_of(k, core), 1).wait()
        product(1, mine, k)

        @pl.when(k < chips - 1)
        def _():
            load(core, chip_of(k + 1, core), 1).start()

        @pl.when(k < 2)
        def _():
            pair(k).wait_recv()

            @pl.loop(0, rows)
            def _(r):
                code, top = encode(mine[k, r] + taken[k, r])
                code_out[k, r] = code
                top_out[k, pl.ds(r, 1), :] = top

            for copy in hop(k, 1):
                copy.start()

    pair(2).wait_recv()
    for copy in hop(0, 1):
        copy.wait_recv()

    @pl.loop(0, rows)
    def _(r):
        came = decode(code_in[0, r], top_in[0, pl.ds(r, 1), :])
        code, top = encode(mine[2, r] + taken[2, r] + came)
        code_out[2, r] = code
        top_out[2, pl.ds(r, 1), :] = top

    for copy in hop(2, 2):
        copy.start()

    pair(3).wait_recv()
    for copy in hop(1, 1):
        copy.wait_recv()

    @pl.loop(0, rows)
    def _(r):
        came = decode(code_in[1, r], top_in[1, pl.ds(r, 1), :])
        mine[3, r] = mine[3, r] + taken[3, r] + came

    for copy in ret_copies:
        copy.wait()

    for copy in hop(2, 2):
        copy.wait_recv()

    @pl.loop(0, rows)
    def _(r):
        came = decode(code_in[2, r], top_in[2, pl.ds(r, 1), :])
        lum[r + 2] = mine[3, r] + came

    def halo(way, i):
        target = (chip + (1 - 2 * way) + chips) % chips * 2 + core
        src, dst = ((halo_out, halo_in), (halo_top_out, halo_top_in))[i]
        return pltpu.make_async_remote_copy(
            src_ref=src.at[way],
            dst_ref=dst.at[way],
            send_sem=halo_sem.at[0, i, way],
            recv_sem=halo_sem.at[1, i, way],
            device_id=at(target),
            device_id_type=MESH,
        )

    def send_halo(way):
        for i in range(2):
            code, top = encode(lum[i + 2 if way else rows + i])
            halo_out[way, i] = code
            halo_top_out[way, i] = top
        for i in range(2):
            halo(way, i).start()

    not_last = chip < chips - 1
    not_first = chip > 0

    @pl.when(not_last)
    def _():
        send_halo(0)

    @pl.when(not_first)
    def _():
        send_halo(1)

    def rate(r):
        return rets[chip * 2 + r // 4, pl.ds(r % 4, 1), :]

    half = rows // 2

    def rate(r):
        return rets[chip * 2 + r // half, pl.ds(r % half, 1), :]

    zero = jnp.zeros((hours, columns), jnp.float32)

    def carry(way, slot, target, i):
        src, dst = ((carry_out, carry_in), (carry_top_out, carry_top_in))[i]
        return pltpu.make_async_remote_copy(
            src_ref=src.at[way],
            dst_ref=dst.at[chip],
            send_sem=carry_sem.at[0, i, target],
            recv_sem=carry_sem.at[1, i, chip],
            device_id=at(target * 2 + core),
            device_id_type=MESH,
        )

    def arrival(source, i):
        src, dst = ((carry_out, carry_in), (carry_top_out, carry_top_in))[i]
        return pltpu.make_async_remote_copy(
            src_ref=src.at[0],
            dst_ref=dst.at[source],
            send_sem=carry_sem.at[0, i, source],
            recv_sem=carry_sem.at[1, i, source],
            device_id=at(source * 2 + core),
            device_id_type=MESH,
        )

    @pl.when(not_last)
    def _():
        down[0] = zero

        @pl.loop(0, rows)
        def _(r):
            down[0] = rate(r) * down[0] + lum[r + 2]

        code, top = encode(down[0])
        carry_out[0] = code
        carry_top_out[0] = top

    @pl.when(not_first)
    def _():
        down[0] = zero

        @pl.loop(0, rows)
        def _(n):
            r = rows - 1 - n
            down[0] = rate(r) * down[0] + lum[r + 2]

        code, top = encode(down[0])
        carry_out[1] = code
        carry_top_out[1] = top

    for target in range(chips):
        @pl.when(target > chip)
        def _():
            for i in range(2):
                carry(0, 0, target, i).start()

        @pl.when(target < chip)
        def _():
            for i in range(2):
                carry(1, 0, target, i).start()

    column = lax.broadcasted_iota(jnp.int32, (hours, columns), 1)

    def blur(row):
        total = binomial_taps[2] * row
        for k in (-2, -1, 1, 2):
            moved = pltpu.roll(row, (-k) % columns, 1)
            inside = column < columns - k if k > 0 else column >= -k
            total = total + binomial_taps[k + 2] * jnp.where(inside, moved, 0.0)
        return total

    @pl.loop(0, rows)
    def _(r):
        mine[0, r] = blur(lum[r + 2])

    @pl.loop(2, rows - 2)
    def _(r):
        total = binomial_taps[2] * mine[0, r]
        for k in (-2, -1, 1, 2):
            total = total + binomial_taps[k + 2] * mine[0, r + k]
        acuity[r] = total

    @pl.when(not_first)
    def _():
        for i in range(2):
            halo(0, i).wait_recv()
        for i in range(2):
            lum[i] = blur(decode(halo_in[0, i], halo_top_in[0, i]))

    @pl.when(chip == 0)
    def _():
        for i in range(2):
            lum[i] = zero

    @pl.when(not_last)
    def _():
        for i in range(2):
            halo(1, i).wait_recv()
        for i in range(2):
            lum[rows + 2 + i] = blur(decode(halo_in[1, i], halo_top_in[1, i]))

    @pl.when(chip == chips - 1)
    def _():
        for i in range(2):
            lum[rows + 2 + i] = zero

    for r in (0, 1, rows - 2, rows - 1):
        total = binomial_taps[2] * mine[0, r]
        for k in (-2, -1, 1, 2):
            source = r + k
            outside = source < 0 or source >= rows
            total = total + binomial_taps[k + 2] * (lum[source + 2] if outside else mine[0, source])
        acuity[r] = total

    def stay(i):
        src, dst = ((acuity, acu_out), (veil, veil_out))[i]
        return pltpu.make_async_copy(
            src.at[pl.ds(core * half, half)], dst.at[:, core], local_sem.at[i]
        )

    def leave(i):
        src, dst = ((acuity, acu_out), (veil, veil_out))[i]
        return pltpu.make_async_remote_copy(
            src_ref=src.at[pl.ds(other * half, half)],
            dst_ref=dst.at[:, core],
            send_sem=out_sem.at[0, i],
            recv_sem=out_sem.at[1, i],
            device_id=at(partner),
            device_id_type=MESH,
        )

    stay(0).start()
    leave(0).start()

    def gain(source):
        total = rets[source * 2, 0:1, :]
        for r in range(1, rows):
            total = total * rets[source * 2 + r // half, r % half : r % half + 1, :]
        return total

    down[0] = zero
    down[1] = zero
    for source in range(chips):
        @pl.when(source < chip)
        def _():
            for i in range(2):
                arrival(source, i).wait_recv()
            down[0] = gain(source) * down[0] + decode(carry_in[source], carry_top_in[source])

    for source in range(chips - 1, -1, -1):
        @pl.when(source > chip)
        def _():
            for i in range(2):
                arrival(source, i).wait_recv()
            down[1] = gain(source) * down[1] + decode(carry_in[source], carry_top_in[source])

    @pl.loop(0, rows)
    def _(r):
        now = rate(r) * down[0] + lum[r + 2]
        down[0] = now
        mine[1, r] = now

    @pl.loop(0, rows)
    def _(n):
        r = rows - 1 - n
        now = rate(r) * down[1] + lum[r + 2]
        down[1] = now
        veil[r] = 0.125 * (mine[1, r] + now)

    stay(1).start()
    leave(1).start()

    @pl.loop(0, chips)
    def _(k):
        pair(k).wait_send()

    for k, n in ((0, 1), (1, 1), (2, 2)):
        for copy in hop(k, n):
            copy.wait_send()

    @pl.when(not_last)
    def _():
        for i in range(2):
            halo(0, i).wait_send()

    @pl.when(not_first)
    def _():
        for i in range(2):
            halo(1, i).wait_send()

    for target in range(chips):
        @pl.when(target > chip)
        def _():
            for i in range(2):
                carry(0, 0, target, i).wait_send()

        @pl.when(target < chip)
        def _():
            for i in range(2):
                carry(1, 0, target, i).wait_send()

    for i in range(2):
        stay(i).wait()
        leave(i).wait()


def fused(coefficients, sky_year, hour_list, retention):
    sky = jnp.take(sky_year, hour_list, axis=1).T
    views, depth, all_rows, columns = coefficients.shape
    hours = sky.shape[0]
    half = retention.shape[0]
    rows = 2 * half
    chips = all_rows // rows
    f32, bf16 = jnp.float32, jnp.bfloat16
    image = (rows, hours, columns)
    out = jax.ShapeDtypeStruct((half, views, hours, columns), f32)
    dma = pltpu.SemaphoreType.DMA
    return pl.pallas_call(
        kernel,
        out_shape=(out, out),
        in_specs=[
            pl.BlockSpec(memory_space=pltpu.VMEM),
            pl.BlockSpec(memory_space=pl.ANY),
            pl.BlockSpec(memory_space=pltpu.VMEM),
        ],
        out_specs=[pl.BlockSpec(memory_space=pl.ANY)] * 2,
        scratch_shapes=[
            pltpu.VMEM((rows * hours, depth * rows), bf16),
            pltpu.VMEM((2, depth, rows, columns), bf16),
            pltpu.VMEM((chips,) + image, f32),
            pltpu.VMEM((chips,) + image, f32),
            pltpu.VMEM((chips,) + image, f32),
            pltpu.VMEM((3,) + image, bf16),
            pltpu.VMEM((3, rows, columns), f32),
            pltpu.VMEM((3,) + image, bf16),
            pltpu.VMEM((3, rows, columns), f32),
            pltpu.VMEM((rows + 4, hours, columns), f32),
            pltpu.VMEM((2, 2, hours, columns), bf16),
            pltpu.VMEM((2, 2, 1, columns), f32),
            pltpu.VMEM((2, 2, hours, columns), bf16),
            pltpu.VMEM((2, 2, 1, columns), f32),
            pltpu.VMEM((2, hours, columns), bf16),
            pltpu.VMEM((2, 1, columns), f32),
            pltpu.VMEM((chips, hours, columns), bf16),
            pltpu.VMEM((chips, 1, columns), f32),
            pltpu.VMEM((2 * chips, half, columns), f32),
            pltpu.VMEM((2, hours, columns), f32),
            pltpu.VMEM(image, f32),
            pltpu.VMEM(image, f32),
            dma((2,)),
            dma((2, 2 * chips)),
            dma((2, chips)),
            dma((2, 2, 3)),
            dma((2, 2, 2)),
            dma((2, 2, chips)),
            dma((2, 2)),
            dma((2,)),
        ],
        compiler_params=pltpu.CompilerParams(
            collective_id=0, has_side_effects=True, vmem_limit_bytes=60 * 1024 * 1024
        ),
    )(sky, coefficients, retention)


def solution(mesh):
    size = mesh.shape["patch"]

    def shards(coefficients, sky_year, hour_list, retention):
        square = size == 8 and coefficients.shape[0] == 2 and retention.shape[0] == 4
        if square:
            return fused(coefficients, sky_year, hour_list, retention)
        return general(coefficients, sky_year, hour_list, retention)

    placed = (P("view", "patch", None, None), P("patch", None), P(), P("patch", None))
    return jax.shard_map(
        shards,
        mesh=mesh,
        in_specs=placed,
        out_specs=(P("patch", "view", None, None), P("patch", "view", None, None)),
        check_vma=False,
    )
```

```python
import jax
import jax.numpy as jnp
from jax import lax
from jax.experimental import pallas as pl
from jax.experimental.pallas import tpu as pltpu
from jax.sharding import PartitionSpec as P

binomial_taps = (0.0625, 0.25, 0.375, 0.25, 0.0625)
MESH = pl.DeviceIdType.MESH
SPAN = 83.0


def padded_2(block, sides, width):
    for axis, dim in sides:
        count = lax.axis_size(axis)
        forward = [(i, i + 1) for i in range(count - 1)]
        backward = [(target, source) for source, target in forward]
        low = lax.ppermute(
            lax.slice_in_dim(block, block.shape[dim] - width, None, axis=dim), axis, forward
        )
        high = lax.ppermute(lax.slice_in_dim(block, 0, width, axis=dim), axis, backward)
        block = jnp.concatenate([low, block, high], axis=dim)
    return block


def entering(value, axis, join, neutral, backward):
    count, mine = (lax.axis_size(axis), lax.axis_index(axis))
    pieces = jax.tree.map(lambda part: lax.all_gather(part, axis), value)
    if backward:
        pieces = jax.tree.map(lambda part: part[::-1], pieces)
        mine = count - 1 - mine
    running = jax.tree.map(
        lambda part, zero: jnp.full_like(part, 0) + jnp.asarray(zero, part.dtype), value, neutral
    )

    def hop(position, running):
        longer = join(running, jax.tree.map(lambda part: part[position], pieces))
        return jax.tree.map(lambda new, old: jnp.where(position < mine, new, old), longer, running)

    return lax.fori_loop(0, count - 1, hop, running)


def combine(earlier, later):
    return (earlier[0] * later[0], later[0] * earlier[1] + later[1])


def taps_sum(padded, axis, length):
    total = jnp.zeros(
        padded.shape[:axis] + (length,) + padded.shape[axis + 1 :],
        jnp.float32,
    )
    for offset in range(5):
        total = total + binomial_taps[offset] * lax.slice_in_dim(
            padded, offset, offset + length, axis=axis
        )
    return total


def general(coefficients, sky_year, hour_list, retention):
    sky_shard_values = jnp.take(sky_year, hour_list, axis=1)
    row_count = retention.shape[0]
    luminance = lax.psum_scatter(
        jnp.einsum(
            "ph,vprc->rvhc", sky_shard_values, coefficients, preferred_element_type=jnp.float32
        ),
        "patch",
        scatter_dimension=0,
        tiled=True,
    )
    padded = padded_2(luminance, (("patch", 0),), 2)
    image_width = padded.shape[3]
    wide_pad = jnp.pad(padded, ((0, 0), (0, 0), (0, 0), (2, 2)))
    across = taps_sum(wide_pad, 3, image_width)
    acuity = taps_sum(across, 0, row_count)
    retain_rates = retention[:, None, None, :]
    front_gain, front_sum = lax.associative_scan(combine, (retain_rates, luminance), axis=0)
    unity = (jnp.ones_like(front_gain[-1]), jnp.zeros_like(front_sum[-1]))
    _, incoming_down = entering((front_gain[-1], front_sum[-1]), "patch", combine, unity, False)
    forward = front_gain * incoming_down[None] + front_sum
    back_gain, back_sum = lax.associative_scan(
        combine, (retain_rates, luminance), reverse=True, axis=0
    )
    _, incoming_up = entering((back_gain[0], back_sum[0]), "patch", combine, unity, True)
    reverse_pass = back_gain * incoming_up[None] + back_sum
    veil = 0.125 * (forward + reverse_pass)
    return (acuity, veil)


def encode(x):
    top = jnp.maximum(jnp.max(jnp.abs(x), axis=0, keepdims=True), 1e-30)
    size = jnp.exp(jnp.abs(x) * (2.0 * SPAN / top) - SPAN)
    return jnp.where(x < 0, -size, size).astype(jnp.bfloat16), top


def decode(code, top):
    y = code.astype(jnp.float32)
    size = (jnp.log(jnp.abs(y)) + SPAN) * (top * (0.5 / SPAN))
    return jnp.where(y < 0, -size, size)


def kernel(
    sky_ref, coef_ref, ret_ref, acu_out, veil_out,
    lhs, held, mine, given, taken,
    code_out, top_out, code_in, top_in, lum,
    halo_out, halo_top_out, halo_in, halo_top_in,
    carry_out, carry_top_out, carry_in, carry_top_in,
    rets, down, acuity, veil,
    load_sem, ret_sem, pair_sem, hop_sem, halo_sem, carry_sem, out_sem, local_sem,
):
    view = lax.axis_index("view")
    me = lax.axis_index("patch")
    devices = 8
    chips = 4
    core = me % 2
    chip = me // 2
    cx = chip % 2
    cy = chip // 2
    other = 1 - core
    depth, rows, columns = held.shape[1:]
    hours = sky_ref.shape[0]

    def at(target):
        return (view, target)

    def chip_of(k, owner):
        fx = (1 - owner) * (1 - k // 2) + owner * (1 - k % 2)
        fy = owner * (1 - k // 2) + (1 - owner) * (1 - k % 2)
        return 2 * (cy + fy * (1 - 2 * cy)) + cx + fx * (1 - 2 * cx)

    def load(v, d, slot):
        return pltpu.make_async_copy(
            coef_ref.at[v, :, pl.ds(pl.multiple_of(d * rows, rows), rows), :],
            held.at[slot],
            load_sem.at[slot],
        )

    load(other, chip_of(0, other), 0).start()
    load(core, chip_of(0, core), 1).start()

    barrier = pltpu.get_barrier_semaphore()
    for step in range(1, devices):
        pl.semaphore_signal(
            barrier, inc=1, device_id=at((me + step) % devices), device_id_type=MESH
        )

    spread = (
        lax.broadcasted_iota(jnp.int32, (depth, depth * rows), 1) // rows
        == lax.broadcasted_iota(jnp.int32, (depth, depth * rows), 0)
    )
    wide = jnp.dot(
        sky_ref[...],
        jnp.where(spread, 1.0, 0.0).astype(jnp.bfloat16),
        preferred_element_type=jnp.float32,
    )
    place = lax.broadcasted_iota(jnp.int32, (hours, depth * rows), 1) % rows
    for r in range(rows):
        lhs[r * hours : (r + 1) * hours, :] = jnp.where(place == r, wide, 0.0).astype(jnp.bfloat16)

    pl.semaphore_wait(barrier, devices - 1)

    rets[me] = ret_ref[...]
    ret_copies = []
    for step in range(1, devices):
        target = (me + step) % devices
        copy = pltpu.make_async_remote_copy(
            src_ref=ret_ref,
            dst_ref=rets.at[me],
            send_sem=ret_sem.at[0, step],
            recv_sem=ret_sem.at[1, step],
            device_id=at(target),
            device_id_type=MESH,
        )
        copy.start()
        ret_copies.append(copy)

    partner = chip * 2 + other
    tile = 256

    def product(slot, dst, k):
        @pl.loop(0, columns // tile)
        def _(t):
            cols = pl.ds(pl.multiple_of(t * tile, tile), tile)
            block = held[slot, :, :, cols].reshape(depth * rows, tile)
            dst[k, :, :, cols] = jnp.dot(
                lhs[...], block, preferred_element_type=jnp.float32
            ).reshape(rows, hours, tile)

    def pair(k):
        return pltpu.make_async_remote_copy(
            src_ref=given.at[k],
            dst_ref=taken.at[k],
            send_sem=pair_sem.at[0, k],
            recv_sem=pair_sem.at[1, k],
            device_id=at(partner),
            device_id_type=MESH,
        )

    def hop(k, n, piece, first, count):
        target = chip_of(n, core) * 2 + core
        return [
            pltpu.make_async_remote_copy(
                src_ref=src.at[k, pl.ds(first, count)],
                dst_ref=dst.at[k, pl.ds(first, count)],
                send_sem=hop_sem.at[0, i, piece],
                recv_sem=hop_sem.at[1, i, piece],
                device_id=at(target),
                device_id_type=MESH,
            )
            for i, (src, dst) in enumerate(((code_out, code_in), (top_out, top_in)))
        ]

    half = rows // 2
    edges = rows - 2

    def hop_half(k, h):
        return hop(k, 1, 2 * k + h, h * half, half)

    second = ((4, 0, 2), (5, edges, 2), (6, 2, rows - 4))

    def unit(k, more):
        load(other, chip_of(k, other), 0).wait()
        product(0, given, k)
        pair(k).start()
        if more:
            load(other, chip_of(k + 1, other), 0).start()
        load(core, chip_of(k, core), 1).wait()
        product(1, mine, k)
        if more:
            load(core, chip_of(k + 1, core), 1).start()

    @pl.loop(0, chips - 1)
    def _(k):
        unit(k, True)

        @pl.when(k < 2)
        def _():
            pair(k).wait_recv()
            for h in range(2):
                @pl.loop(h * half, h * half + half)
                def _(r):
                    code, top = encode(mine[k, r] + taken[k, r])
                    code_out[k, r] = code
                    top_out[k, r] = top

                for copy in hop_half(k, h):
                    copy.start()

    pair(2).wait_recv()
    for piece, first, count in second:
        if piece < 6:
            for copy in hop_half(0, piece - 4):
                copy.wait_recv()

        @pl.loop(first, first + count)
        def _(r):
            came = decode(code_in[0, r], top_in[0, r])
            code, top = encode(mine[2, r] + taken[2, r] + came)
            code_out[2, r] = code
            top_out[2, r] = top

        for copy in hop(2, 2, piece, first, count):
            copy.start()

    unit(chips - 1, False)
    pair(3).wait_recv()
    for h in range(2):
        for copy in hop_half(1, h):
            copy.wait_recv()

        @pl.loop(h * half, h * half + half)
        def _(r):
            came = decode(code_in[1, r], top_in[1, r])
            mine[3, r] = mine[3, r] + taken[3, r] + came

    for copy in ret_copies:
        copy.wait()

    def halo(way, i):
        target = (chip + (1 - 2 * way) + chips) % chips * 2 + core
        src, dst = ((halo_out, halo_in), (halo_top_out, halo_top_in))[i]
        return pltpu.make_async_remote_copy(
            src_ref=src.at[way],
            dst_ref=dst.at[way],
            send_sem=halo_sem.at[0, i, way],
            recv_sem=halo_sem.at[1, i, way],
            device_id=at(target),
            device_id_type=MESH,
        )

    def send_halo(way):
        for i in range(2):
            code, top = encode(lum[i + 2 if way else rows + i])
            halo_out[way, i] = code
            halo_top_out[way, i] = top
        for i in range(2):
            halo(way, i).start()

    not_last = chip < chips - 1
    not_first = chip > 0

    for piece, first, count in second:
        for copy in hop(2, 2, piece, first, count):
            copy.wait_recv()

        @pl.loop(first, first + count)
        def _(r):
            came = decode(code_in[2, r], top_in[2, r])
            lum[r + 2] = mine[3, r] + came

        if piece < 6:
            @pl.when(not_last if piece == 5 else not_first)
            def _():
                send_halo(5 - piece)

    def rate(r):
        return rets[chip * 2 + r // half, pl.ds(r % half, 1), :]

    zero = jnp.zeros((hours, columns), jnp.float32)

    def carry(way, slot, target, i):
        src, dst = ((carry_out, carry_in), (carry_top_out, carry_top_in))[i]
        return pltpu.make_async_remote_copy(
            src_ref=src.at[way],
            dst_ref=dst.at[chip],
            send_sem=carry_sem.at[0, i, target],
            recv_sem=carry_sem.at[1, i, chip],
            device_id=at(target * 2 + core),
            device_id_type=MESH,
        )

    def arrival(source, i):
        src, dst = ((carry_out, carry_in), (carry_top_out, carry_top_in))[i]
        return pltpu.make_async_remote_copy(
            src_ref=src.at[0],
            dst_ref=dst.at[source],
            send_sem=carry_sem.at[0, i, source],
            recv_sem=carry_sem.at[1, i, source],
            device_id=at(source * 2 + core),
            device_id_type=MESH,
        )

    @pl.when(not_last)
    def _():
        down[0] = zero

        @pl.loop(0, rows)
        def _(r):
            down[0] = rate(r) * down[0] + lum[r + 2]

        code, top = encode(down[0])
        carry_out[0] = code
        carry_top_out[0] = top

    @pl.when(not_first)
    def _():
        down[0] = zero

        @pl.loop(0, rows)
        def _(n):
            r = rows - 1 - n
            down[0] = rate(r) * down[0] + lum[r + 2]

        code, top = encode(down[0])
        carry_out[1] = code
        carry_top_out[1] = top

    for target in range(chips):
        @pl.when(target > chip)
        def _():
            for i in range(2):
                carry(0, 0, target, i).start()

        @pl.when(target < chip)
        def _():
            for i in range(2):
                carry(1, 0, target, i).start()

    column = lax.broadcasted_iota(jnp.int32, (hours, columns), 1)

    def blur(row):
        total = binomial_taps[2] * row
        for k in (-2, -1, 1, 2):
            moved = pltpu.roll(row, (-k) % columns, 1)
            inside = column < columns - k if k > 0 else column >= -k
            total = total + binomial_taps[k + 2] * jnp.where(inside, moved, 0.0)
        return total

    @pl.loop(0, rows)
    def _(r):
        mine[0, r] = blur(lum[r + 2])

    @pl.loop(2, rows - 2)
    def _(r):
        total = binomial_taps[2] * mine[0, r]
        for k in (-2, -1, 1, 2):
            total = total + binomial_taps[k + 2] * mine[0, r + k]
        acuity[r] = total

    @pl.when(not_first)
    def _():
        for i in range(2):
            halo(0, i).wait_recv()
        for i in range(2):
            lum[i] = blur(decode(halo_in[0, i], halo_top_in[0, i]))

    @pl.when(chip == 0)
    def _():
        for i in range(2):
            lum[i] = zero

    @pl.when(not_last)
    def _():
        for i in range(2):
            halo(1, i).wait_recv()
        for i in range(2):
            lum[rows + 2 + i] = blur(decode(halo_in[1, i], halo_top_in[1, i]))

    @pl.when(chip == chips - 1)
    def _():
        for i in range(2):
            lum[rows + 2 + i] = zero

    for r in (0, 1, rows - 2, rows - 1):
        total = binomial_taps[2] * mine[0, r]
        for k in (-2, -1, 1, 2):
            source = r + k
            outside = source < 0 or source >= rows
            total = total + binomial_taps[k + 2] * (lum[source + 2] if outside else mine[0, source])
        acuity[r] = total

    def stay(i):
        src, dst = ((acuity, acu_out), (veil, veil_out))[i]
        return pltpu.make_async_copy(
            src.at[pl.ds(core * half, half)], dst.at[:, core], local_sem.at[i]
        )

    def leave(i):
        src, dst = ((acuity, acu_out), (veil, veil_out))[i]
        return pltpu.make_async_remote_copy(
            src_ref=src.at[pl.ds(other * half, half)],
            dst_ref=dst.at[:, core],
            send_sem=out_sem.at[0, i],
            recv_sem=out_sem.at[1, i],
            device_id=at(partner),
            device_id_type=MESH,
        )

    stay(0).start()
    leave(0).start()

    def gain(source):
        total = rets[source * 2, 0:1, :]
        for r in range(1, rows):
            total = total * rets[source * 2 + r // half, r % half : r % half + 1, :]
        return total

    down[0] = zero
    down[1] = zero
    for source in range(chips):
        @pl.when(source < chip)
        def _():
            for i in range(2):
                arrival(source, i).wait_recv()
            down[0] = gain(source) * down[0] + decode(carry_in[source], carry_top_in[source])

    for source in range(chips - 1, -1, -1):
        @pl.when(source > chip)
        def _():
            for i in range(2):
                arrival(source, i).wait_recv()
            down[1] = gain(source) * down[1] + decode(carry_in[source], carry_top_in[source])

    @pl.loop(0, rows)
    def _(r):
        now = rate(r) * down[0] + lum[r + 2]
        down[0] = now
        mine[1, r] = now

    @pl.loop(0, rows)
    def _(n):
        r = rows - 1 - n
        now = rate(r) * down[1] + lum[r + 2]
        down[1] = now
        veil[r] = 0.125 * (mine[1, r] + now)

    stay(1).start()
    leave(1).start()

    @pl.loop(0, chips)
    def _(k):
        pair(k).wait_send()

    for k in range(2):
        for h in range(2):
            for copy in hop_half(k, h):
                copy.wait_send()

    for piece, first, count in second:
        for copy in hop(2, 2, piece, first, count):
            copy.wait_send()

    @pl.when(not_last)
    def _():
        for i in range(2):
            halo(0, i).wait_send()

    @pl.when(not_first)
    def _():
        for i in range(2):
            halo(1, i).wait_send()

    for target in range(chips):
        @pl.when(target > chip)
        def _():
            for i in range(2):
                carry(0, 0, target, i).wait_send()

        @pl.when(target < chip)
        def _():
            for i in range(2):
                carry(1, 0, target, i).wait_send()

    for i in range(2):
        stay(i).wait()
        leave(i).wait()


def fused(coefficients, sky_year, hour_list, retention):
    year = lax.broadcasted_iota(jnp.int32, (hour_list.shape[0], sky_year.shape[1]), 1)
    picks = (year == hour_list[:, None]).astype(jnp.bfloat16)
    sky = jnp.einsum(
        "hy,py->hp", picks, sky_year, preferred_element_type=jnp.float32
    ).astype(jnp.bfloat16)
    views, depth, all_rows, columns = coefficients.shape
    hours = sky.shape[0]
    half = retention.shape[0]
    rows = 2 * half
    chips = all_rows // rows
    f32, bf16 = jnp.float32, jnp.bfloat16
    image = (rows, hours, columns)
    out = jax.ShapeDtypeStruct((half, views, hours, columns), f32)
    dma = pltpu.SemaphoreType.DMA
    return pl.pallas_call(
        kernel,
        out_shape=(out, out),
        in_specs=[
            pl.BlockSpec(memory_space=pltpu.VMEM),
            pl.BlockSpec(memory_space=pl.ANY),
            pl.BlockSpec(memory_space=pltpu.VMEM),
        ],
        out_specs=[pl.BlockSpec(memory_space=pl.ANY)] * 2,
        scratch_shapes=[
            pltpu.VMEM((rows * hours, depth * rows), bf16),
            pltpu.VMEM((2, depth, rows, columns), bf16),
            pltpu.VMEM((chips,) + image, f32),
            pltpu.VMEM((chips,) + image, f32),
            pltpu.VMEM((chips,) + image, f32),
            pltpu.VMEM((3,) + image, bf16),
            pltpu.VMEM((3, rows, 1, columns), f32),
            pltpu.VMEM((3,) + image, bf16),
            pltpu.VMEM((3, rows, 1, columns), f32),
            pltpu.VMEM((rows + 4, hours, columns), f32),
            pltpu.VMEM((2, 2, hours, columns), bf16),
            pltpu.VMEM((2, 2, 1, columns), f32),
            pltpu.VMEM((2, 2, hours, columns), bf16),
            pltpu.VMEM((2, 2, 1, columns), f32),
            pltpu.VMEM((2, hours, columns), bf16),
            pltpu.VMEM((2, 1, columns), f32),
            pltpu.VMEM((chips, hours, columns), bf16),
            pltpu.VMEM((chips, 1, columns), f32),
            pltpu.VMEM((2 * chips, half, columns), f32),
            pltpu.VMEM((2, hours, columns), f32),
            pltpu.VMEM(image, f32),
            pltpu.VMEM(image, f32),
            dma((2,)),
            dma((2, 2 * chips)),
            dma((2, chips)),
            dma((2, 2, 7)),
            dma((2, 2, 2)),
            dma((2, 2, chips)),
            dma((2, 2)),
            dma((2,)),
        ],
        compiler_params=pltpu.CompilerParams(
            collective_id=0, has_side_effects=True, vmem_limit_bytes=48 * 1024 * 1024
        ),
    )(sky, coefficients, retention)


def solution(mesh):
    size = mesh.shape["patch"]

    def shards(coefficients, sky_year, hour_list, retention):
        square = size == 8 and coefficients.shape[0] == 2 and retention.shape[0] == 4
        if square:
            return fused(coefficients, sky_year, hour_list, retention)
        return general(coefficients, sky_year, hour_list, retention)

    placed = (P("view", "patch", None, None), P("patch", None), P(), P("patch", None))
    return jax.shard_map(
        shards,
        mesh=mesh,
        in_specs=placed,
        out_specs=(P("patch", "view", None, None), P("patch", "view", None, None)),
        check_vma=False,
    )
```
